32 devices in a mesh: dp: 8 (over z, core), expert: 4 (over y, x).
Axes of the slice: x: 2, y: 2, z: 4, core: 2. Of those that a mesh axis runs over, the one named last changes fastest.
Arguments:
- tokens: bfloat16 [128, 3584], P(('dp', 'expert')), may hold values from -6 to 6
- routes: int32 [128, 1], P(('dp', 'expert')), may hold values from 0 to 1; in each aligned block of 4 rows (0 to 3, 4 to 7, ...) at most 4 rows name the same one
- route_gates: float32 [128, 1], P(('dp', 'expert')), may hold values from 0.1 to 0.6
- out_grad: bfloat16 [128, 3584], P(('dp', 'expert')), may hold values from -6 to 6
- w_gate: bfloat16 [3584, 2048], P(None, 'expert'), may hold values from -0.09375 to 0.09375
- w_up: bfloat16 [3584, 2048], P(None, 'expert'), may hold values from -0.09375 to 0.09375
- w_down: bfloat16 [2048, 3584], P('expert'), may hold values from -0.1875 to 0.1875
Outputs:
- moe_out: bfloat16 [128, 3584], P(('dp', 'expert'))
- token_grad: bfloat16 [128, 3584], P(('dp', 'expert'))
- grad_gate: bfloat16 [3584, 2048], P('dp', 'expert')
- grad_up: bfloat16 [3584, 2048], P('dp', 'expert')
- grad_down: bfloat16 [2048, 3584], P('expert', 'dp')
The draws below stay inside these ranges and needn't reach their ends.
Inputs may be any that keep to these rules, and one draw needn't show every extreme that they name: `routes`: each row names 1 different experts; among the rows of one device no expert is named by more than 4 rows, a bound that some block reaches.
All inputs are finite; a program needn't handle non-finite values.
Results may differ from the reference program's by a relative error of at most 0.02.
Values may be sent and summed in bfloat16 or wider, within the bound.
No kernel may reach another device: no remote copies, remote signals or barrier semaphores. Data moves between devices by JAX's collectives and lax.ppermute only.
A program may use at most 64 MiB of HBM per device.

```python
import math
import jax
import jax.numpy as jnp
import numpy as np
from jax import lax

D = 3584
FF_WIN = 1024
TOK_DEV = 4
SLICES = 2
FF_DEV = 512
EXPERTS = 2
TOPK = 1
CAP = 4
TOKENS = 128
N_EXPERT = 4


def levels(rng, dims, pieces, smallest, top_value):
    def one(axis_at, parts):
        steps = jax.random.uniform(jax.random.fold_in(jax.random.fold_in(rng, 6), axis_at), (parts,), jnp.float32, smallest / len(pieces), top_value / len(pieces))
        return jnp.repeat(jnp.exp(steps), dims[axis_at] // parts).reshape((-1,) + (1,) * (len(dims) - axis_at - 1))

    factor_of = one(*pieces[0])
    for cut in pieces[1:]:
        factor_of = factor_of * one(*cut)
    return factor_of


def shared_out(own_key, own, number, rows, count, top, limit, skew):
    order = jax.random.permutation(own_key, count)
    packed, common = shares(count, rows * top, limit, skew, True), shares(count, rows * top, limit, skew, False)
    places = jnp.arange(count)

    def named(lengths, rotation):
        used = int((lengths > 0).sum())
        fixed = max(1, used // 4)
        moved = fixed + (places - fixed + rotation * (used - fixed)) % max(1, count - fixed)
        return jnp.zeros((count,), jnp.int32).at[order[jnp.where(places < fixed, places, moved)]].set(jnp.asarray(lengths, jnp.int32))

    lengths = jnp.where(number % 4 == 0, named(packed, number // 4), named(common, number - number // 4 - 1))
    mixed = jax.random.permutation(jax.random.fold_in(own, 3), count)
    giver, receiver = mixed[0:count // 2 * 2:2], mixed[1:count // 2 * 2:2]
    slack = jnp.minimum(lengths[giver] - 1, limit - lengths[receiver]) // 2
    slack = jnp.where((giver == order[0]) | (receiver == order[0]) | (lengths[receiver] == 0), 0, jnp.maximum(slack, 0))
    moved = jax.random.randint(jax.random.fold_in(own, 4), (count // 2,), 0, 1 << 20) % (slack + 1)
    lengths = lengths.at[giver].add(-moved).at[receiver].add(moved)
    labels = jnp.searchsorted(jnp.cumsum(lengths), jnp.arange(rows * top), side="right").astype(jnp.int32)
    grid = labels.reshape(top, rows).T
    grid = grid[jax.random.permutation(jax.random.fold_in(own, 1), rows)]
    rotation = jax.random.randint(jax.random.fold_in(own, 2), (rows, 1), 0, top)
    return jnp.take_along_axis(grid, (jnp.arange(top)[None, :] + rotation) % top, axis=1)


def shares(amount, total, reach, lean, full):
    loads = [(1 << 20) // math.isqrt(rank ** lean) + 1 for rank in range(1, amount + 1)]
    largest = reach if full else min(reach, max(-(-total // amount), total * loads[0] // sum(loads)))
    least = 1 if total - largest >= amount - 1 else 0
    holding, spare = [largest] + [least] * (amount - 1), total - largest - least * (amount - 1)
    while spare > 0:
        candidates = [i for i in range(1, amount) if holding[i] < largest] or [i for i in range(1, amount) if holding[i] < reach]
        whole, left = sum([loads[i] for i in candidates]), spare
        for i in candidates:
            addition = min(reach - holding[i], max(1, left * loads[i] // whole), spare)
            holding[i] = holding[i] + addition
            spare = spare - addition
    return np.array(holding)


def bell_draw(key, shape, width, limit, shards=(), held_as=jnp.bfloat16):
    values = width * jax.random.normal(key, shape, jnp.float32)
    if shards:
        values = values * levels(key, shape, shards, -0.22, 0.18)
    return jnp.clip(values, -limit, limit).astype(held_as)


def setup_inputs(seed: int = 0) -> dict:
    key_list = jax.random.split(jax.random.key(seed), 8)
    tokens = bell_draw(key_list[0], (TOKENS, D), 1.0, 6.0, ((0, 32),))
    routes_keys = jax.random.split(jax.random.fold_in(key_list[1], 1), TOKENS // TOK_DEV)
    routes_turns = jax.random.permutation(jax.random.fold_in(key_list[1], 3), TOKENS // TOK_DEV)
    routes = jax.vmap(lambda own, number: shared_out(jax.random.fold_in(key_list[1], 2), own, number, TOK_DEV, EXPERTS, TOPK, CAP, 2))(routes_keys, routes_turns).reshape((TOKENS, TOPK))
    route_gates = jnp.clip(0.1 + 0.5 * jax.random.uniform(key_list[2], (TOKENS, TOPK), jnp.float32) ** levels(key_list[2], (TOKENS, TOPK), ((0, 32),), -0.2, 0.2), 0.1, 0.6)
    out_grad = bell_draw(key_list[3], (TOKENS, D), 1.0, 6.0, ((0, 32),))
    w_gate = bell_draw(key_list[4], (D, EXPERTS * FF_WIN), D ** -0.5, 0.09375, ((1, 4),))
    w_up = bell_draw(key_list[5], (D, EXPERTS * FF_WIN), D ** -0.5, 0.09375, ((1, 4),))
    w_down = bell_draw(key_list[6], (EXPERTS * FF_WIN, D), FF_WIN ** -0.5, 0.1875, ((0, 4),))
    return {"tokens": tokens, "routes": routes, "route_gates": route_gates, "out_grad": out_grad, "w_gate": w_gate, "w_up": w_up, "w_down": w_down}


def expert_pass(rows, slot_grad, wg, wu, wd):
    a = jnp.dot(rows, wg, preferred_element_type=jnp.float32)
    b = jnp.dot(rows, wu, preferred_element_type=jnp.float32)
    sig = jax.nn.sigmoid(a)
    act = a * sig
    hidden = (act * b).astype(jnp.bfloat16)
    out = jnp.dot(hidden, wd, preferred_element_type=jnp.float32).astype(jnp.bfloat16)
    d_hidden = jnp.dot(slot_grad, wd.T, preferred_element_type=jnp.float32)
    d_up = (d_hidden * act).astype(jnp.bfloat16)
    d_gate = (d_hidden * b * sig * (1.0 + a * (1.0 - sig))).astype(jnp.bfloat16)
    d_rows = (jnp.dot(d_gate, wg.T, preferred_element_type=jnp.float32) + jnp.dot(d_up, wu.T, preferred_element_type=jnp.float32)).astype(jnp.bfloat16)
    part_gate = jnp.dot(rows.T, d_gate, preferred_element_type=jnp.float32).astype(jnp.bfloat16).astype(jnp.float32)
    part_up = jnp.dot(rows.T, d_up, preferred_element_type=jnp.float32).astype(jnp.bfloat16).astype(jnp.float32)
    part_down = jnp.dot(hidden.T, slot_grad, preferred_element_type=jnp.float32).astype(jnp.bfloat16).astype(jnp.float32)
    return out, d_rows, part_gate, part_up, part_down


def reference(tokens, routes, route_gates, out_grad, w_gate, w_up, w_down):
    group_rows = TOK_DEV * N_EXPERT
    rows_cap = N_EXPERT * CAP
    groups = TOKENS // group_rows
    xg = tokens.reshape(groups, group_rows, D)
    rg = routes.reshape(groups, group_rows, TOPK)
    gg = route_gates.reshape(groups, group_rows, TOPK)
    dg = out_grad.reshape(groups, group_rows, D)
    wg4 = w_gate.reshape(D, EXPERTS, SLICES, FF_DEV).transpose(1, 2, 0, 3)
    wu4 = w_up.reshape(D, EXPERTS, SLICES, FF_DEV).transpose(1, 2, 0, 3)
    wd4 = w_down.reshape(EXPERTS, SLICES, FF_DEV, D)

    def group_step(carry, inputs):
        xgr, rgr, ggr, dgr = inputs

        def per_expert(expert_id):
            hit = rgr == expert_id
            chosen = jnp.any(hit, axis=1)
            gate = jnp.sum(jnp.where(hit, ggr, jnp.float32(0.0)), axis=1)
            iota = jnp.arange(group_rows, dtype=jnp.int32)
            keys = jnp.where(chosen, iota, iota + group_rows)
            order = jnp.argsort(keys)[:rows_cap].astype(jnp.int32)
            valid = chosen[order]
            gate_rows = jnp.where(valid, gate[order], jnp.float32(0.0))
            rows = xgr[order]
            slot_grad = (gate_rows[:, None] * dgr[order].astype(jnp.float32)).astype(jnp.bfloat16)

            def per_slice(slice_id):
                return expert_pass(rows, slot_grad, wg4[expert_id, slice_id], wu4[expert_id, slice_id], wd4[expert_id, slice_id])

            outs, drows, pg, pu, pd = lax.map(per_slice, jnp.arange(SLICES, dtype=jnp.int32))
            back_out = gate_rows[:, None] * jnp.sum(outs.astype(jnp.float32), axis=0)
            back_dx = jnp.where(valid[:, None], jnp.sum(drows.astype(jnp.float32), axis=0), jnp.float32(0.0))
            return order, back_out, back_dx, pg, pu, pd

        orders, back_out, back_dx, pg, pu, pd = lax.map(per_expert, jnp.arange(EXPERTS, dtype=jnp.int32))
        flat = orders.reshape(-1)
        tok_out = jnp.zeros((group_rows, D), jnp.float32).at[flat].add(back_out.reshape(-1, D))
        tok_dx = jnp.zeros((group_rows, D), jnp.float32).at[flat].add(back_dx.reshape(-1, D))
        return (carry[0] + pg, carry[1] + pu, carry[2] + pd), (tok_out, tok_dx)

    start = (jnp.zeros((EXPERTS, SLICES, D, FF_DEV), jnp.float32), jnp.zeros((EXPERTS, SLICES, D, FF_DEV), jnp.float32), jnp.zeros((EXPERTS, SLICES, FF_DEV, D), jnp.float32))
    sums, (outs, dxs) = lax.scan(group_step, start, (xg, rg, gg, dg))
    moe_out = outs.reshape(TOKENS, D).astype(jnp.bfloat16)
    token_grad = dxs.reshape(TOKENS, D).astype(jnp.bfloat16)
    grad_gate = sums[0].transpose(2, 0, 1, 3).reshape(D, EXPERTS * FF_WIN).astype(jnp.bfloat16)
    grad_up = sums[1].transpose(2, 0, 1, 3).reshape(D, EXPERTS * FF_WIN).astype(jnp.bfloat16)
    grad_down = sums[2].reshape(EXPERTS * FF_WIN, D).astype(jnp.bfloat16)
    return moe_out, token_grad, grad_gate, grad_up, grad_down
```

```python
import jax
import jax.numpy as jnp
from jax import lax
from jax.sharding import PartitionSpec as P


def dot(a, b, ca, cb):
    return lax.dot_general(a, b, (((ca,), (cb,)), ((), ())), preferred_element_type=jnp.float32)


def local(tokens, routes, route_gates, out_grad, w_gate, w_up, w_down):
    n_ex, n_dp = lax.axis_size("expert"), lax.axis_size("dp")
    slices = min(8, n_ex // 2)
    n_experts = n_ex // slices
    rows, width = tokens.shape
    block = width // n_dp
    hidden_dim = w_gate.shape[1]
    bf, f32 = jnp.bfloat16, jnp.float32

    expert_ids = jnp.arange(n_experts, dtype=jnp.int32)
    hit = routes[:, :, None] == expert_ids[None, None, :]
    gates = jnp.sum(jnp.where(hit, route_gates[:, :, None], f32(0.0)), axis=1)
    gates = jnp.repeat(gates.T, slices, axis=0)

    both = jnp.concatenate(
        [tokens.reshape(rows, n_dp, block), out_grad.reshape(rows, n_dp, block)], axis=2
    ).transpose(1, 0, 2)
    send_cols = (both.astype(f32)[:, None] * gates[None, :, :, None]).astype(bf)
    cols = lax.all_to_all(
        send_cols.reshape(n_dp * n_ex, rows, 2 * block), ("dp", "expert"), 0, 0, tiled=True
    ).reshape(n_dp * n_ex * rows, 2 * block)

    pair = lax.all_gather(jnp.concatenate([tokens, out_grad], axis=1), "expert", tiled=True)
    x, og = pair[:, :width], pair[:, width:]

    a = dot(x, w_gate, 1, 0)
    b = dot(x, w_up, 1, 0)
    sig = jax.nn.sigmoid(a)
    act = a * sig
    hidden = (act * b).astype(bf)
    dh = dot(og, w_down, 1, 1)
    d_up = (dh * act).astype(bf)
    d_gate = (dh * b * sig * (1.0 + a * (1.0 - sig))).astype(bf)
    factors = lax.all_gather(jnp.concatenate([d_gate, d_up, hidden], axis=1), "dp", tiled=True)
    out = dot(hidden, w_down, 1, 0).astype(bf)
    dx = (dot(d_gate, w_gate, 1, 1) + dot(d_up, w_up, 1, 1)).astype(bf)
    back = lax.all_to_all(
        jnp.concatenate([out, dx], axis=1).reshape(n_ex, rows, 2 * width), "expert", 0, 0, tiled=True
    )
    home = jnp.sum(back.astype(f32) * gates[:, :, None], axis=0).astype(bf)

    grad_gate_up = dot(cols[:, :block], factors[:, : 2 * hidden_dim], 0, 0).astype(bf)
    grad_down = dot(factors[:, 2 * hidden_dim :], cols[:, block:], 0, 0).astype(bf)
    return (
        home[:, :width],
        home[:, width:],
        grad_gate_up[:, :hidden_dim],
        grad_gate_up[:, hidden_dim:],
        grad_down,
    )


def solution(mesh):
    both = P(("dp", "expert"), None)
    return jax.shard_map(
        local,
        mesh=mesh,
        in_specs=(both, both, both, both, P(None, "expert"), P(None, "expert"), P("expert", None)),
        out_specs=(both, both, P("dp", "expert"), P("dp", "expert"), P("expert", "dp")),
        check_vma=False,
    )
```

```python
import functools

import jax
import jax.numpy as jnp
from jax import lax
from jax.experimental import pallas as pl
from jax.experimental.pallas import tpu as pltpu
from jax.sharding import PartitionSpec as P


BF, F32 = jnp.bfloat16, jnp.float32
VMEM = pl.BlockSpec(memory_space=pltpu.VMEM)
HBM = pl.BlockSpec(memory_space=pl.ANY)
SMEM = pl.BlockSpec(memory_space=pltpu.SMEM)
LANES = 128
PIECES = 3
LOADS = 4


def dot(a, b, ca, cb):
    return lax.dot_general(a, b, (((ca,), (cb,)), ((), ())), preferred_element_type=F32)


def near(*arrays):
    return [pltpu.with_memory_space_constraint(x, pltpu.VMEM) for x in arrays]


def far(*arrays):
    return [pltpu.with_memory_space_constraint(x, pltpu.HBM) for x in arrays]


def call(kernel, n_in, outs, scratch=(), in_specs=None, out_specs=None):
    return pl.pallas_call(
        kernel,
        out_shape=outs,
        in_specs=in_specs or [VMEM] * n_in,
        out_specs=out_specs or [VMEM] * len(outs),
        scratch_shapes=scratch,
        compiler_params=pltpu.CompilerParams(vmem_limit_bytes=16 << 20),
    )


def n_slices():
    return min(8, lax.axis_size("expert") // 2)


def pack_kernel(tokens, routes, gates, out_grad, pair, sems):
    rows, width = tokens.shape
    copies = [
        pltpu.make_async_copy(src, pair.at[:, pl.ds(j * width, width)], sems.at[j])
        for j, src in enumerate((tokens, out_grad))
    ]
    for c in copies:
        c.start()
    row = lax.broadcasted_iota(jnp.int32, (rows, LANES), 0)
    lane = lax.broadcasted_iota(jnp.int32, (rows, LANES), 1)
    tail = jnp.zeros((rows, LANES), F32)
    for e in range(lax.axis_size("expert") // n_slices()):
        rest = jnp.zeros((rows, LANES), F32)
        for t in range(rows):
            for k in range(routes.shape[0]):
                gate = jnp.where(routes[k, t] == e, gates[k, t], F32(0.0))
                rest = rest + jnp.where(row == t, gate, F32(0.0))
        for p in range(PIECES):
            piece = rest.astype(BF).astype(F32)
            tail = jnp.where(lane == PIECES * e + p, piece, tail)
            rest = rest - piece
    pair[:, 2 * width :] = tail.astype(BF)
    for c in copies:
        c.wait()


def load_kernel(*refs):
    n = (len(refs) - 1) // 2
    sems = refs[-1]
    copies = []
    for k in range(n):
        step = refs[k].shape[0] // LOADS
        for j in range(LOADS):
            cut = pl.ds(j * step, step)
            copies.append(
                pltpu.make_async_copy(refs[k].at[cut], refs[n + k].at[cut], sems.at[k, j])
            )
    for c in copies:
        c.start()
    for c in copies:
        c.wait()


def first_kernel(n, n_z, *refs):
    pairs, (wg, wu, wd), outs, pair = refs[:n], refs[n : n + 3], refs[n + 3 : -1], refs[-1]
    rows, (width, h) = pairs[0].shape[0], wg.shape
    for k in range(n):
        pair[pl.ds(k * rows, rows), :] = pairs[k][...]
    tail = pair[:, 2 * width :].astype(F32)
    lane = lax.broadcasted_iota(jnp.int32, tail.shape, 1)
    low = PIECES * lax.div(lax.axis_index("expert"), n_slices())
    gate = jnp.sum(
        jnp.where((lane >= low) & (lane < low + PIECES), tail, F32(0.0)), axis=1, keepdims=True
    )
    x = pair[:, :width]
    a = dot(x, wg[...], 1, 0)
    b = dot(x, wu[...], 1, 0)
    dh = dot(pair[:, width : 2 * width], wd[...], 1, 1) * gate
    sig = jax.nn.sigmoid(a)
    act = a * sig
    d_gate = (dh * b * sig * (1.0 + a * (1.0 - sig))).astype(BF)
    d_up = (dh * act).astype(BF)
    hidden = (act * b * gate).astype(BF)
    for k, out in enumerate(outs):
        out[:, :h] = d_gate
        out[:, h : 2 * h] = d_up
        out[:, 2 * h : 3 * h] = hidden
        if n_z:
            z = lax.div(lax.axis_index("dp"), 2) ^ k
            size = width // n_z
            for j in range(2):
                start = pl.multiple_of(j * width + z * size, LANES)
                out[:, 3 * h + j * size : 3 * h + (j + 1) * size] = pair[:, pl.ds(start, size)]


def second_kernel(n, f, wg, wu, wd, *outs):
    h, width = wd.shape
    rows = outs[0].shape[0]
    o = dot(f[:, 2 * h : 3 * h], wd[...], 1, 0).astype(BF)
    dx = (dot(f[:, :h], wg[...], 1, 1) + dot(f[:, h : 2 * h], wu[...], 1, 1)).astype(BF)
    for k in range(n):
        outs[k][:, :width] = o[k * rows : (k + 1) * rows]
        outs[k][:, width:] = dx[k * rows : (k + 1) * rows]


def grad_kernel(*refs):
    n = len(refs) - 6
    parts, (gg, gu, gd, f, x, og) = refs[:n], refs[n:]
    block, h = gg.shape
    rows = parts[0].shape[0]
    first = lax.rem(lax.axis_index("dp"), 2) == 0
    for k in range(n):
        cut = pl.ds(k * rows, rows)
        f[cut, :] = parts[k][:, : 3 * h]
        for j, dst in enumerate((x, og)):
            low = 3 * h + 2 * j * block
            dst[cut, :] = jnp.where(
                first,
                parts[k][:, low : low + block],
                parts[k][:, low + block : low + 2 * block],
            )
    grads = dot(x[...], f[:, : 2 * h], 0, 0)
    gg[...] = grads[:, :h].astype(BF)
    gu[...] = grads[:, h:].astype(BF)
    gd[...] = dot(og[...], f[:, 2 * h :], 0, 0).astype(BF)


def swap(x, axis, s):
    return lax.ppermute(x, axis, [(i, i ^ s) for i in range(lax.axis_size(axis))])


def local(tokens, routes, route_gates, out_grad, w_gate, w_up, w_down):
    n_ex, n_dp = lax.axis_size("expert"), lax.axis_size("dp")
    rows, width = tokens.shape
    h = w_gate.shape[1]
    n_z, block = n_dp // 2, width // n_dp
    permutes = n_ex <= 4 and n_dp <= 8 and (2 * block) % LANES == 0
    n = n_ex if permutes else 1
    part = rows * n_ex // n
    group = rows * n_ex
    wide = 2 * width + LANES
    weights = (w_gate, w_up, w_down)
    x, og, *weights = far(tokens, out_grad, *weights)
    (pair,) = call(
        pack_kernel,
        4,
        [pltpu.VMEM((rows, wide), BF)],
        [pltpu.SemaphoreType.DMA((2,))],
        in_specs=[HBM, SMEM, SMEM, HBM],
    )(x, routes.T, route_gates.T, og)
    weights = call(
        load_kernel,
        3,
        [pltpu.VMEM(w.shape, BF) for w in weights],
        [pltpu.SemaphoreType.DMA((3, LOADS))],
        in_specs=[HBM] * 3,
    )(*weights)
    if permutes:
        pairs = [pair]
        for s in range(1, n_ex):
            pairs.append(swap(pair, "expert", s))
    else:
        pairs = [lax.all_gather(pair, "expert", tiled=True)]
    sizes = [3 * h + 4 * block] * n_z if permutes else [3 * h]
    factors = call(
        functools.partial(first_kernel, n, n_z if permutes else 0),
        n + 3,
        [pltpu.VMEM((group, size), BF) for size in sizes],
        [pltpu.VMEM((group, wide), BF)],
    )(*near(*pairs, *weights))
    if permutes:
        parts = [factors[0]]
        for s in range(1, n_z):
            parts.append(swap(factors[s], "dp", 2 * s))
        for s in range(n_z):
            parts.append(swap(parts[s], "dp", 1))
    else:
        factor_rows = lax.all_gather(factors[0], "dp", tiled=True)
        cols = pairs[0][:, : 2 * width].reshape(group, 2, n_dp, block).transpose(2, 0, 1, 3)
        cols = lax.all_to_all(cols, "dp", 0, 0, tiled=True).reshape(n_dp * group, 2 * block)
    outs = call(
        functools.partial(second_kernel, n), 4, [pltpu.VMEM((part, 2 * width), BF)] * n
    )(*near(factors[0], *weights))
    if permutes:
        back = [outs[0]]
        for s in range(1, n_ex):
            back.append(swap(outs[s], "expert", s))
        grad_gate, grad_up, grad_down = call(
            grad_kernel,
            2 * n_z,
            [jax.ShapeDtypeStruct((block, h), BF)] * 3,
            [
                pltpu.VMEM((n_dp * group, 3 * h), BF),
                pltpu.VMEM((n_dp * group, block), BF),
                pltpu.VMEM((n_dp * group, block), BF),
            ],
        )(*near(*parts))
    else:
        back = lax.all_to_all(outs[0].reshape(n_ex, rows, 2 * width), "expert", 0, 0, tiled=True)
        back = [back[e] for e in range(n_ex)]
        both = dot(cols[:, :block], factor_rows[:, : 2 * h], 0, 0).astype(BF)
        grad_gate, grad_up = both[:, :h], both[:, h:]
        grad_down = dot(cols[:, block:], factor_rows[:, 2 * h :], 0, 0).astype(BF)
    moe_out, token_grad = [
        sum(part[:, cut].astype(F32) for part in back).astype(BF)
        for cut in (slice(0, width), slice(width, None))
    ]
    return moe_out, token_grad, grad_gate, grad_up, grad_down.T


def solution(mesh):
    both = P(("dp", "expert"), None)
    return jax.shard_map(
        local,
        mesh=mesh,
        in_specs=(both, both, both, both, P(None, "expert"), P(None, "expert"), P("expert", None)),
        out_specs=(both, both, P("dp", "expert"), P("dp", "expert"), P("expert", "dp")),
        check_vma=False,
    )
```

```python
import functools

import jax
import jax.numpy as jnp
from jax import lax
from jax.experimental import pallas as pl
from jax.experimental.pallas import tpu as pltpu
from jax.sharding import PartitionSpec as P


BF, F32 = jnp.bfloat16, jnp.float32
VMEM = pl.BlockSpec(memory_space=pltpu.VMEM)
HBM = pl.BlockSpec(memory_space=pl.ANY)
LANES = 128
PIECES = 3
TURN = 512
PREFETCH = pl.CostEstimate(flops=10**13, transcendentals=0, bytes_accessed=10**9)


def dot(a, b, ca, cb):
    return lax.dot_general(a, b, (((ca,), (cb,)), ((), ())), preferred_element_type=F32)


def near(*arrays):
    return [pltpu.with_memory_space_constraint(x, pltpu.VMEM) for x in arrays]


def far(*arrays):
    return [pltpu.with_memory_space_constraint(x, pltpu.HBM) for x in arrays]


def call(kernel, n_in, outs, scratch=(), in_specs=None, out_specs=None, cost=None):
    return pl.pallas_call(
        kernel,
        cost_estimate=cost,
        out_shape=outs,
        in_specs=in_specs or [VMEM] * n_in,
        out_specs=out_specs or [VMEM] * len(outs),
        scratch_shapes=scratch,
        compiler_params=pltpu.CompilerParams(vmem_limit_bytes=16 << 20),
    )


def n_slices():
    return min(8, lax.axis_size("expert") // 2)


def pack_kernel(tokens, routes_hbm, gates_hbm, out_grad, pair, routes, gates, sems):
    rows, width = tokens.shape
    small = [
        pltpu.make_async_copy(routes_hbm, routes, sems.at[2]),
        pltpu.make_async_copy(gates_hbm, gates, sems.at[3]),
    ]
    copies = [
        pltpu.make_async_copy(src, pair.at[:, pl.ds(j * width, width)], sems.at[j])
        for j, src in enumerate((tokens, out_grad))
    ]
    for c in small + copies:
        c.start()
    for c in small:
        c.wait()
    row = lax.broadcasted_iota(jnp.int32, (rows, LANES), 0)
    lane = lax.broadcasted_iota(jnp.int32, (rows, LANES), 1)
    tail = jnp.zeros((rows, LANES), F32)
    for e in range(lax.axis_size("expert") // n_slices()):
        rest = jnp.zeros((rows, LANES), F32)
        for t in range(rows):
            for k in range(routes.shape[0]):
                gate = jnp.where(routes[k, t] == e, gates[k, t], F32(0.0))
                rest = rest + jnp.where(row == t, gate, F32(0.0))
        for p in range(PIECES):
            piece = rest.astype(BF).astype(F32)
            tail = jnp.where(lane == PIECES * e + p, piece, tail)
            rest = rest - piece
    pair[:, 2 * width :] = tail.astype(BF)
    for c in copies:
        c.wait()


def turn_kernel(*refs):
    n = len(refs) // 2
    for w, t in zip(refs[:n], refs[n:]):
        for low in range(0, w.shape[0], TURN):
            cut = pl.ds(low, min(TURN, w.shape[0] - low))
            t[:, cut] = w[cut, :].T


def first_kernel(n, n_z, *refs):
    pairs, (wg, wu, wd_t), outs, pair = refs[:n], refs[n : n + 3], refs[n + 3 : -1], refs[-1]
    rows, (width, h) = pairs[0].shape[0], wg.shape
    for k in range(n):
        pair[pl.ds(k * rows, rows), :] = pairs[k][...]
    tail = pair[:, 2 * width :].astype(F32)
    lane = lax.broadcasted_iota(jnp.int32, tail.shape, 1)
    low = PIECES * lax.div(lax.axis_index("expert"), n_slices())
    gate = jnp.sum(
        jnp.where((lane >= low) & (lane < low + PIECES), tail, F32(0.0)), axis=1, keepdims=True
    )
    a = dot(pair[:, :width], wg[...], 1, 0)
    b = dot(pair[:, :width], wu[...], 1, 0)
    dh = dot(pair[:, width : 2 * width], wd_t[...], 1, 0) * gate
    sig = jax.nn.sigmoid(a)
    act = a * sig
    d_gate = (dh * b * sig * (1.0 + a * (1.0 - sig))).astype(BF)
    d_up = (dh * act).astype(BF)
    hidden = (act * b * gate).astype(BF)
    for k, out in enumerate(outs):
        out[:, :h] = d_gate
        out[:, h : 2 * h] = d_up
        out[:, 2 * h : 3 * h] = hidden
        if n_z:
            z = lax.div(lax.axis_index("dp"), 2) ^ k
            size = width // n_z
            for j in range(2):
                start = pl.multiple_of(j * width + z * size, LANES)
                out[:, 3 * h + j * size : 3 * h + (j + 1) * size] = pair[:, pl.ds(start, size)]


def second_kernel(n, f, wg_t, wu_t, wd, *outs):
    h, width = wd.shape
    rows = outs[0].shape[0]
    o = dot(f[:, 2 * h : 3 * h], wd[...], 1, 0).astype(BF)
    dx = (dot(f[:, :h], wg_t[...], 1, 0) + dot(f[:, h : 2 * h], wu_t[...], 1, 0)).astype(BF)
    for k in range(n):
        outs[k][:, :width] = o[k * rows : (k + 1) * rows]
        outs[k][:, width:] = dx[k * rows : (k + 1) * rows]


def grad_kernel(n, *refs):
    parts, outs, (f, x, og), stage, sems = refs[:n], refs[n : n + 3], refs[-7:-4], refs[-4:-1], refs[-1]
    block, h = stage[0].shape
    rows = parts[0].shape[0]
    first = lax.rem(lax.axis_index("dp"), 2) == 0
    for k in range(n):
        cut = pl.ds(k * rows, rows)
        f[cut, :] = parts[k][:, : 3 * h]
        for j, dst in enumerate((x, og)):
            low = 3 * h + 2 * j * block
            dst[cut, :] = jnp.where(
                first,
                parts[k][:, low : low + block],
                parts[k][:, low + block : low + 2 * block],
            )
    copies = [pltpu.make_async_copy(stage[k], outs[k], sems.at[k]) for k in range(3)]
    for k, rows_ref in enumerate((x, x, og)):
        stage[k][...] = dot(rows_ref[...], f[:, k * h : (k + 1) * h], 0, 0).astype(BF)
        copies[k].start()
    for c in copies:
        c.wait()


def home_kernel(n, *refs):
    back, outs, stage, sems = refs[:n], refs[n : n + 2], refs[n + 2 : n + 4], refs[-1]
    width = stage[0].shape[1]
    copies = [pltpu.make_async_copy(stage[k], outs[k], sems.at[k]) for k in range(2)]
    for k in range(2):
        cut = slice(k * width, (k + 1) * width)
        total = back[0][:, cut].astype(F32)
        for part in back[1:]:
            total = total + part[:, cut].astype(F32)
        stage[k][...] = total.astype(BF)
        copies[k].start()
    for c in copies:
        c.wait()


def swap(x, axis, s):
    return lax.ppermute(x, axis, [(i, i ^ s) for i in range(lax.axis_size(axis))])


def local(tokens, routes, route_gates, out_grad, w_gate, w_up, w_down):
    n_ex, n_dp = lax.axis_size("expert"), lax.axis_size("dp")
    rows, width = tokens.shape
    h = w_gate.shape[1]
    n_z, block = n_dp // 2, width // n_dp
    permutes = n_ex <= 4 and n_dp <= 8 and (2 * block) % LANES == 0
    n = n_ex if permutes else 1
    part = rows * n_ex // n
    group = rows * n_ex
    wide = 2 * width + LANES
    x, og, route_rows, gate_rows = far(tokens, out_grad, routes.T, route_gates.T)
    (pair,) = call(
        pack_kernel,
        4,
        [pltpu.VMEM((rows, wide), BF)],
        [
            pltpu.SMEM(route_rows.shape, jnp.int32),
            pltpu.SMEM(gate_rows.shape, F32),
            pltpu.SemaphoreType.DMA((4,)),
        ],
        in_specs=[HBM] * 4,
        cost=PREFETCH,
    )(x, route_rows, gate_rows, og)
    weights = (w_gate, w_up, w_down)
    wg_t, wu_t, wd_t = call(turn_kernel, 3, [pltpu.VMEM(w.shape[::-1], BF) for w in weights])(
        *near(*weights)
    )
    if permutes:
        pairs = [pair]
        for s in range(1, n_ex):
            pairs.append(swap(pair, "expert", s))
    else:
        pairs = [lax.all_gather(pair, "expert", tiled=True)]
    sizes = [3 * h + 4 * block] * n_z if permutes else [3 * h]
    factors = call(
        functools.partial(first_kernel, n, n_z if permutes else 0),
        n + 3,
        [pltpu.VMEM((group, size), BF) for size in sizes],
        [pltpu.VMEM((group, wide), BF)],
    )(*near(*pairs, w_gate, w_up, wd_t))
    if permutes:
        parts = [factors[0]]
        for s in range(1, n_z):
            parts.append(swap(factors[s], "dp", 2 * s))
        for s in range(n_z):
            parts.append(swap(parts[s], "dp", 1))
    else:
        factor_rows = lax.all_gather(factors[0], "dp", tiled=True)
        cols = pairs[0][:, : 2 * width].reshape(group, 2, n_dp, block).transpose(2, 0, 1, 3)
        cols = lax.all_to_all(cols, "dp", 0, 0, tiled=True).reshape(n_dp * group, 2 * block)
    outs = call(
        functools.partial(second_kernel, n), 4, [pltpu.VMEM((part, 2 * width), BF)] * n
    )(*near(factors[0], wg_t, wu_t, w_down))
    if permutes:
        back = [outs[0]]
        for s in range(1, n_ex):
            back.append(swap(outs[s], "expert", s))
        total = n_dp * group
        grad_gate, grad_up, grad_down = call(
            functools.partial(grad_kernel, len(parts)),
            len(parts),
            [pltpu.HBM((block, h), BF)] * 3,
            [pltpu.VMEM((total, size), BF) for size in (3 * h, block, block)]
            + [pltpu.VMEM((block, h), BF)] * 3
            + [pltpu.SemaphoreType.DMA((3,))],
            out_specs=[HBM] * 3,
        )(*near(*parts))
        moe_out, token_grad = call(
            functools.partial(home_kernel, n),
            n,
            [pltpu.HBM((rows, width), BF)] * 2,
            [pltpu.VMEM((rows, width), BF)] * 2 + [pltpu.SemaphoreType.DMA((2,))],
            out_specs=[HBM] * 2,
        )(*near(*back))
    else:
        back = lax.all_to_all(outs[0].reshape(n_ex, rows, 2 * width), "expert", 0, 0, tiled=True)
        back = [back[e] for e in range(n_ex)]
        both = dot(cols[:, :block], factor_rows[:, : 2 * h], 0, 0).astype(BF)
        grad_gate, grad_up = both[:, :h], both[:, h:]
        grad_down = dot(cols[:, block:], factor_rows[:, 2 * h :], 0, 0).astype(BF)
        moe_out, token_grad = [
            sum(part[:, cut].astype(F32) for part in back).astype(BF)
            for cut in (slice(0, width), slice(width, None))
        ]
    return moe_out, token_grad, grad_gate, grad_up, grad_down.T


def solution(mesh):
    both = P(("dp", "expert"), None)
    return jax.shard_map(
        local,
        mesh=mesh,
        in_specs=(both, both, both, both, P(None, "expert"), P(None, "expert"), P("expert", None)),
        out_specs=(both, both, P("dp", "expert"), P("dp", "expert"), P("expert", "dp")),
        check_vma=False,
    )
```

```python
import functools

import jax
import jax.numpy as jnp
from jax import lax
from jax.experimental import pallas as pl
from jax.experimental.pallas import tpu as pltpu
from jax.sharding import PartitionSpec as P


BF, F32 = jnp.bfloat16, jnp.float32
VMEM = pl.BlockSpec(memory_space=pltpu.VMEM)
HBM = pl.BlockSpec(memory_space=pl.ANY)
LANES = 128
PIECES = 3
TURN = 512
PREFETCH = pl.CostEstimate(flops=10**13, transcendentals=0, bytes_accessed=10**9)


def dot(a, b, ca, cb):
    return lax.dot_general(a, b, (((ca,), (cb,)), ((), ())), preferred_element_type=F32)


def near(*arrays):
    return [pltpu.with_memory_space_constraint(x, pltpu.VMEM) for x in arrays]


def far(*arrays):
    return [pltpu.with_memory_space_constraint(x, pltpu.HBM) for x in arrays]


def call(kernel, n_in, outs, scratch=(), in_specs=None, out_specs=None, cost=None):
    return pl.pallas_call(
        kernel,
        cost_estimate=cost,
        out_shape=outs,
        in_specs=in_specs or [VMEM] * n_in,
        out_specs=out_specs or [VMEM] * len(outs),
        scratch_shapes=scratch,
        compiler_params=pltpu.CompilerParams(vmem_limit_bytes=16 << 20),
    )


def n_slices():
    return min(8, lax.axis_size("expert") // 2)


def pack_kernel(tokens, routes_hbm, gates_hbm, out_grad, pair, routes, gates, sems):
    rows, width = tokens.shape
    small = [
        pltpu.make_async_copy(routes_hbm, routes, sems.at[2]),
        pltpu.make_async_copy(gates_hbm, gates, sems.at[3]),
    ]
    copies = [
        pltpu.make_async_copy(src, pair.at[:, pl.ds(j * width, width)], sems.at[j])
        for j, src in enumerate((tokens, out_grad))
    ]
    for c in small + copies:
        c.start()
    for c in small:
        c.wait()
    row = lax.broadcasted_iota(jnp.int32, (rows, LANES), 0)
    lane = lax.broadcasted_iota(jnp.int32, (rows, LANES), 1)
    tail = jnp.zeros((rows, LANES), F32)
    for e in range(lax.axis_size("expert") // n_slices()):
        rest = jnp.zeros((rows, LANES), F32)
        for t in range(rows):
            for k in range(routes.shape[0]):
                gate = jnp.where(routes[k, t] == e, gates[k, t], F32(0.0))
                rest = rest + jnp.where(row == t, gate, F32(0.0))
        for p in range(PIECES):
            piece = rest.astype(BF).astype(F32)
            tail = jnp.where(lane == PIECES * e + p, piece, tail)
            rest = rest - piece
    pair[:, 2 * width :] = tail.astype(BF)
    for c in copies:
        c.wait()


def turn_kernel(*refs):
    n = len(refs) // 2
    for w, t in zip(refs[:n], refs[n:]):
        for low in range(0, w.shape[0], TURN):
            cut = pl.ds(low, min(TURN, w.shape[0] - low))
            t[:, cut] = w[cut, :].T


def first_kernel(n, n_z, *refs):
    pairs, (wg, wu, wd_t), outs, pair = refs[:n], refs[n : n + 3], refs[n + 3 : -1], refs[-1]
    rows, (width, h) = pairs[0].shape[0], wg.shape
    for k in range(n):
        pair[pl.ds(k * rows, rows), :] = pairs[k][...]
    tail = pair[:, 2 * width :].astype(F32)
    lane = lax.broadcasted_iota(jnp.int32, tail.shape, 1)
    low = PIECES * lax.div(lax.axis_index("expert"), n_slices())
    gate = jnp.sum(
        jnp.where((lane >= low) & (lane < low + PIECES), tail, F32(0.0)), axis=1, keepdims=True
    )
    a = dot(pair[:, :width], wg[...], 1, 0)
    b = dot(pair[:, :width], wu[...], 1, 0)
    dh = dot(pair[:, width : 2 * width], wd_t[...], 1, 0) * gate
    sig = jax.nn.sigmoid(a)
    act = a * sig
    d_gate = (dh * b * sig * (1.0 + a * (1.0 - sig))).astype(BF)
    d_up = (dh * act).astype(BF)
    hidden = (act * b * gate).astype(BF)
    for k, out in enumerate(outs):
        out[:, :h] = d_gate
        out[:, h : 2 * h] = d_up
        out[:, 2 * h : 3 * h] = hidden
        if n_z:
            z = lax.div(lax.axis_index("dp"), 2) ^ k
            size = width // n_z
            for j in range(2):
                start = pl.multiple_of(j * width + z * size, LANES)
                out[:, 3 * h + j * size : 3 * h + (j + 1) * size] = pair[:, pl.ds(start, size)]


def second_kernel(n, f, wg_t, wu_t, wd, *outs):
    h, width = wd.shape
    rows = outs[0].shape[0]
    o = dot(f[:, 2 * h : 3 * h], wd[...], 1, 0).astype(BF)
    dx = (dot(f[:, :h], wg_t[...], 1, 0) + dot(f[:, h : 2 * h], wu_t[...], 1, 0)).astype(BF)
    for k in range(n):
        outs[k][:, :width] = o[k * rows : (k + 1) * rows]
        outs[k][:, width:] = dx[k * rows : (k + 1) * rows]


def place(parts, low_row, f, x, og):
    h, block, rows = f.shape[1] // 3, x.shape[1], parts[0].shape[0]
    first = lax.rem(lax.axis_index("dp"), 2) == 0
    for k, part in enumerate(parts):
        cut = pl.ds(low_row + k * rows, rows)
        f[cut, :] = part[:, : 3 * h]
        for j, dst in enumerate((x, og)):
            low = 3 * h + 2 * j * block
            dst[cut, :] = jnp.where(
                first, part[:, low : low + block], part[:, low + block : low + 2 * block]
            )


def early_kernel(*refs):
    place(refs[:-3], 0, *refs[-3:])


def grad_kernel(n, *refs):
    early, parts, outs = refs[:3], refs[3 : n + 3], refs[n + 3 : n + 6]
    placed, stage, sems = refs[-7:-4], refs[-4:-1], refs[-1]
    h, ready = stage[0].shape[1], early[0].shape[0]
    for src, dst in zip(early, placed):
        dst[:ready, :] = src[...]
    place(parts, ready, *placed)
    f, x, og = placed
    copies = [pltpu.make_async_copy(stage[k], outs[k], sems.at[k]) for k in range(3)]
    for k, rows_ref in enumerate((x, x, og)):
        stage[k][...] = dot(rows_ref[...], f[:, k * h : (k + 1) * h], 0, 0).astype(BF)
        copies[k].start()
    for c in copies:
        c.wait()


def home_kernel(n, *refs):
    back, outs, stage, sems = refs[:n], refs[n : n + 2], refs[n + 2 : n + 4], refs[-1]
    width = stage[0].shape[1]
    copies = [pltpu.make_async_copy(stage[k], outs[k], sems.at[k]) for k in range(2)]
    for k in range(2):
        cut = slice(k * width, (k + 1) * width)
        total = back[0][:, cut].astype(F32)
        for part in back[1:]:
            total = total + part[:, cut].astype(F32)
        stage[k][...] = total.astype(BF)
        copies[k].start()
    for c in copies:
        c.wait()


def swap(x, axis, s):
    return lax.ppermute(x, axis, [(i, i ^ s) for i in range(lax.axis_size(axis))])


def local(tokens, routes, route_gates, out_grad, w_gate, w_up, w_down):
    n_ex, n_dp = lax.axis_size("expert"), lax.axis_size("dp")
    rows, width = tokens.shape
    h = w_gate.shape[1]
    n_z, block = n_dp // 2, width // n_dp
    permutes = n_ex <= 4 and n_dp <= 8 and (2 * block) % LANES == 0
    n = n_ex if permutes else 1
    part = rows * n_ex // n
    group = rows * n_ex
    wide = 2 * width + LANES
    x, og, route_rows, gate_rows = far(tokens, out_grad, routes.T, route_gates.T)
    (pair,) = call(
        pack_kernel,
        4,
        [pltpu.VMEM((rows, wide), BF)],
        [
            pltpu.SMEM(route_rows.shape, jnp.int32),
            pltpu.SMEM(gate_rows.shape, F32),
            pltpu.SemaphoreType.DMA((4,)),
        ],
        in_specs=[HBM] * 4,
        cost=PREFETCH,
    )(x, route_rows, gate_rows, og)
    weights = (w_gate, w_up, w_down)
    wg_t, wu_t, wd_t = call(turn_kernel, 3, [pltpu.VMEM(w.shape[::-1], BF) for w in weights])(
        *near(*weights)
    )
    if permutes:
        pairs = [pair]
        for s in range(1, n_ex):
            pairs.append(swap(pair, "expert", s))
    else:
        pairs = [lax.all_gather(pair, "expert", tiled=True)]
    sizes = [3 * h + 4 * block] * n_z if permutes else [3 * h]
    factors = call(
        functools.partial(first_kernel, n, n_z if permutes else 0),
        n + 3,
        [pltpu.VMEM((group, size), BF) for size in sizes],
        [pltpu.VMEM((group, wide), BF)],
    )(*near(*pairs, w_gate, w_up, wd_t))
    if permutes:
        parts = [factors[0]]
        for s in range(1, n_z):
            parts.append(swap(factors[s], "dp", 2 * s))
        for s in range(n_z):
            parts.append(swap(parts[s], "dp", 1))
    else:
        factor_rows = lax.all_gather(factors[0], "dp", tiled=True)
        cols = pairs[0][:, : 2 * width].reshape(group, 2, n_dp, block).transpose(2, 0, 1, 3)
        cols = lax.all_to_all(cols, "dp", 0, 0, tiled=True).reshape(n_dp * group, 2 * block)
    outs = call(
        functools.partial(second_kernel, n), 4, [pltpu.VMEM((part, 2 * width), BF)] * n
    )(*near(factors[0], wg_t, wu_t, w_down))
    if permutes:
        back = [outs[0]]
        for s in range(1, n_ex):
            back.append(swap(outs[s], "expert", s))
        total = n_dp * group
        ready = (n_z + 1) * group
        early = call(
            early_kernel, n_z + 1, [pltpu.VMEM((ready, size), BF) for size in (3 * h, block, block)]
        )(*near(*parts[: n_z + 1]))
        grad_gate, grad_up, grad_down = call(
            functools.partial(grad_kernel, n_z - 1),
            n_z + 2,
            [pltpu.HBM((block, h), BF)] * 3,
            [pltpu.VMEM((total, size), BF) for size in (3 * h, block, block)]
            + [pltpu.VMEM((block, h), BF)] * 3
            + [pltpu.SemaphoreType.DMA((3,))],
            out_specs=[HBM] * 3,
        )(*near(*early, *parts[n_z + 1 :]))
        moe_out, token_grad = call(
            functools.partial(home_kernel, n),
            n,
            [pltpu.HBM((rows, width), BF)] * 2,
            [pltpu.VMEM((rows, width), BF)] * 2 + [pltpu.SemaphoreType.DMA((2,))],
            out_specs=[HBM] * 2,
        )(*near(*back))
    else:
        back = lax.all_to_all(outs[0].reshape(n_ex, rows, 2 * width), "expert", 0, 0, tiled=True)
        back = [back[e] for e in range(n_ex)]
        both = dot(cols[:, :block], factor_rows[:, : 2 * h], 0, 0).astype(BF)
        grad_gate, grad_up = both[:, :h], both[:, h:]
        grad_down = dot(cols[:, block:], factor_rows[:, 2 * h :], 0, 0).astype(BF)
        moe_out, token_grad = [
            sum(part[:, cut].astype(F32) for part in back).astype(BF)
            for cut in (slice(0, width), slice(width, None))
        ]
    return moe_out, token_grad, grad_gate, grad_up, grad_down.T


def solution(mesh):
    both = P(("dp", "expert"), None)
    return jax.shard_map(
        local,
        mesh=mesh,
        in_specs=(both, both, both, both, P(None, "expert"), P(None, "expert"), P("expert", None)),
        out_specs=(both, both, P("dp", "expert"), P("dp", "expert"), P("expert", "dp")),
        check_vma=False,
    )
```
